32 devices in a mesh: ctx: 8 (over z, x), ch: 4 (over y, core).
Axes of the slice: x: 2, y: 2, z: 4, core: 2. Of those that a mesh axis runs over, the one named last changes fastest.
Arguments:
- conv_input: bfloat16 [128, 1024], P('ch', 'ctx'), may hold values from -6 to 6
- gate_value: bfloat16 [128, 1024], P('ch', 'ctx'), may hold values from -6 to 6
- out_grad: bfloat16 [128, 1024], P('ch', 'ctx'), may hold values from -6 to 6
- long_filter: bfloat16 [128, 1024], P('ch', 'ctx'), may hold values from -4 to 4
- skip_bias: float32 [128], P('ch'), may hold values from 0.5 to 1.5
- short_weight: float32 [128, 3], P('ch'), may hold values from -3.5 to 3.5
Outputs:
- input_grad: bfloat16 [128, 1024], P('ch', 'ctx')
- filter_grad: float32 [128, 1024], P('ch', 'ctx')
The draws below stay inside these ranges and needn't reach their ends.
All inputs are finite; a program needn't handle non-finite values.
Results may differ from the reference program's by a relative error of at most 0.007.
Values may be sent and summed in bfloat16 or wider, within the bound.
A program may use at most 64 MiB of HBM per device.

```python
import jax
import jax.numpy as jnp

KS = 3
FEATURE_TOTAL = 128
SEQUENCE_SPAN = 1024


def draw_long_filter(key, part):
    sampler_seeds = jax.random.split(key, 7)
    slow_share = 0.5
    delay_location = jnp.arange(SEQUENCE_SPAN, dtype=jnp.float32)[None, :]
    is_slow = jax.random.uniform(sampler_seeds[0], (FEATURE_TOTAL, 1)) < slow_share
    slow_rate = jnp.exp(jax.random.uniform(sampler_seeds[1], (FEATURE_TOTAL, 1), minval=jnp.log(0.2), maxval=jnp.log(2.0))) / SEQUENCE_SPAN
    fast_rate = jnp.exp(jax.random.uniform(sampler_seeds[2], (FEATURE_TOTAL, 1), minval=jnp.log(1.0 / 50.0), maxval=jnp.log(1.0 / 30.0)))
    rate = jnp.where(is_slow, slow_rate, fast_rate)
    spike_location = jax.random.uniform(sampler_seeds[3], (FEATURE_TOTAL, 3)) * SEQUENCE_SPAN
    spike_multiplier = jax.random.uniform(sampler_seeds[4], (FEATURE_TOTAL, 3), minval=0.5, maxval=0.8)
    damping_exponent = -rate * delay_location
    for spike_slot_number in range(3):
        damping_exponent = damping_exponent + jnp.where(delay_location > spike_location[:, spike_slot_number:spike_slot_number + 1], jnp.log(spike_multiplier[:, spike_slot_number:spike_slot_number + 1]), 0.0)
    effective = jnp.expm1(-2.0 * rate * SEQUENCE_SPAN) / jnp.expm1(-2.0 * rate)
    scale_row = effective ** (-0.5)
    rough = jnp.clip(jax.random.normal(sampler_seeds[6], (FEATURE_TOTAL, SEQUENCE_SPAN)), -4.0, 4.0)
    taps = rough * scale_row * jnp.exp(damping_exponent)
    return taps.astype(jnp.float32).astype(jnp.bfloat16)


def block_scale(own_key, extent, shards, low, top_value):
    def one(axis_at, parts):
        steps = jax.random.uniform(jax.random.fold_in(jax.random.fold_in(own_key, 6), axis_at), (parts,), jnp.float32, low / len(shards), top_value / len(shards))
        return jnp.repeat(jnp.exp(steps), extent[axis_at] // parts).reshape((-1,) + (1,) * (len(extent) - axis_at - 1))

    loudness = one(*shards[0])
    for cut in shards[1:]:
        loudness = loudness * one(*cut)
    return loudness


def noise(own_key, dims, scale, limit, pieces=(), kind=jnp.bfloat16):
    values = scale * jax.random.normal(own_key, dims, jnp.float32)
    if pieces:
        values = values * block_scale(own_key, dims, pieces, -0.22, 0.18)
    return jnp.clip(values, -limit, limit).astype(kind)


def setup_inputs(seed: int = 0) -> dict:
    key_list = jax.random.split(jax.random.key(seed), 7)
    return {
        "conv_input": noise(key_list[0], (FEATURE_TOTAL, SEQUENCE_SPAN), 1.0, 6.0, ((0, 4), (1, 8))),
        "gate_value": noise(key_list[1], (FEATURE_TOTAL, SEQUENCE_SPAN), 1.0, 6.0, ((0, 4), (1, 8))),
        "out_grad": noise(key_list[2], (FEATURE_TOTAL, SEQUENCE_SPAN), 1.0, 6.0, ((0, 4), (1, 8))),
        "long_filter": draw_long_filter(jax.random.fold_in(key_list[6], 71), 0),
        "skip_bias": jnp.clip(0.5 + 1.0 * jax.random.uniform(key_list[4], (FEATURE_TOTAL,), jnp.float32) ** block_scale(key_list[4], (FEATURE_TOTAL,), ((0, 4),), -0.2, 0.2), 0.5, 1.5),
        "short_weight": noise(key_list[5], (FEATURE_TOTAL, KS), KS ** -0.5, 3.5, ((0, 4),), jnp.float32),
    }


def reference(conv_input, gate_value, out_grad, long_filter, skip_bias, short_weight):
    conv_grad = (gate_value.astype(jnp.float32) * out_grad.astype(jnp.float32)).astype(jnp.bfloat16)
    grad_full = conv_grad.astype(jnp.float32)
    length_fft = 2 * SEQUENCE_SPAN
    spec_grad = jnp.fft.rfft(grad_full, n=length_fft, axis=1)
    spec_filter = jnp.fft.rfft(long_filter.astype(jnp.float32), n=length_fft, axis=1)
    spec_input = jnp.fft.rfft(conv_input.astype(jnp.float32), n=length_fft, axis=1)
    correlated = jnp.fft.irfft(jnp.conj(spec_filter) * spec_grad, n=length_fft, axis=1)[:, :SEQUENCE_SPAN]
    mid_grad = (correlated.astype(jnp.float32) + skip_bias[:, None] * grad_full).astype(jnp.bfloat16)
    padded = jnp.pad(mid_grad.astype(jnp.float32), ((0, 0), (0, KS - 1)))
    input_grad = jnp.zeros((FEATURE_TOTAL, SEQUENCE_SPAN), jnp.float32)
    for tap_index in range(KS):
        input_grad = input_grad + short_weight[:, tap_index:tap_index + 1] * padded[:, tap_index:tap_index + SEQUENCE_SPAN]
    lagged = jnp.fft.irfft(jnp.conj(spec_input) * spec_grad, n=length_fft, axis=1)[:, :SEQUENCE_SPAN]
    filter_grad = lagged.astype(jnp.float32) * (1.0 / (SEQUENCE_SPAN ** 0.5))
    return input_grad.astype(jnp.bfloat16), filter_grad
```

```python
import functools
import math

import jax
import jax.numpy as jnp
from jax import lax
from jax.experimental import pallas as pl
from jax.experimental.pallas import tpu as pltpu
from jax.sharding import PartitionSpec as P


def from_behind(value, axis, steps):
    count = lax.axis_size(axis)
    initial, last = (max(0, -steps), min(count, count - steps))
    return lax.ppermute(value, axis, [(source, source + steps) for source in range(initial, last)])


def packed_tables(block_len):
    span_len = 2 * block_len
    sample_idx = jnp.arange(span_len, dtype=jnp.int32)[:, None]
    freq_idx = jnp.arange(block_len + 1, dtype=jnp.int32)[None, :]
    angle_fwd = 2.0 * math.pi / span_len * (sample_idx * freq_idx % span_len).astype(jnp.float32)
    forward = jnp.concatenate([jnp.cos(angle_fwd), -jnp.sin(angle_fwd[:, 1:block_len])], axis=1)
    column_idx = jnp.arange(span_len, dtype=jnp.int32)[None, :]
    real_freq = jnp.arange(block_len + 1, dtype=jnp.int32)[:, None]
    real_weight = jnp.where((real_freq == 0) | (real_freq == block_len), 1.0, 2.0) / span_len
    angle_real = 2.0 * math.pi / span_len * (real_freq * column_idx % span_len).astype(jnp.float32)
    imag_freq = jnp.arange(1, block_len, dtype=jnp.int32)[:, None]
    angle_imag = 2.0 * math.pi / span_len * (imag_freq * column_idx % span_len).astype(jnp.float32)
    inverse = jnp.concatenate(
        [real_weight * jnp.cos(angle_real), -2.0 / span_len * jnp.sin(angle_imag)], axis=0
    )
    return (forward, inverse)


def split_table(table):
    upper = table.astype(jnp.bfloat16)
    lower = (table - upper.astype(jnp.float32)).astype(jnp.bfloat16)
    return (upper, lower)


def split_dot(data, parts):
    return jnp.dot(data, parts[0], preferred_element_type=jnp.float32) + jnp.dot(
        data, parts[1], preferred_element_type=jnp.float32
    )


def conj_times(first, second, block_len):
    zero_col = jnp.zeros(first.shape[:-1] + (1,), jnp.float32)
    first_re = first[..., : block_len + 1]
    first_im = jnp.concatenate([zero_col, first[..., block_len + 1 :], zero_col], axis=-1)
    second_re = second[..., : block_len + 1]
    second_im = jnp.concatenate([zero_col, second[..., block_len + 1 :], zero_col], axis=-1)
    prod_re = first_re * second_re + first_im * second_im
    prod_im = first_re * second_im - first_im * second_re
    return jnp.concatenate([prod_re, prod_im[..., 1:block_len]], axis=-1)


def spectral_dot(left, right):
    return jnp.dot(left, right, precision=lax.Precision.HIGH, preferred_element_type=jnp.float32)


def general_device(conv_input, gate_value, out_grad, long_filter, skip_bias, short_weight):
    channels = conv_input.shape[0]
    block_len = conv_input.shape[1]
    span_len = 2 * block_len
    shards = lax.axis_size("ctx")
    own_index = lax.axis_index("ctx")
    forward, inverse = packed_tables(block_len)
    forward_parts = split_table(forward)
    head_parts = split_table(forward[:block_len])
    conv_grad = (gate_value.astype(jnp.float32) * out_grad.astype(jnp.float32)).astype(jnp.bfloat16)
    whole_filter = lax.all_gather(long_filter, "ctx", axis=1, tiled=True)
    padded_filter = jnp.concatenate(
        [jnp.zeros((channels, block_len), jnp.bfloat16), whole_filter], axis=1
    )

    def mid_term(grad_block, block_idx):
        first_col = jnp.clip(block_idx - own_index, 0, shards - 1) * block_len
        segment = lax.dynamic_slice_in_dim(padded_filter, first_col, span_len, 1)
        grad_spec = split_dot(grad_block, head_parts)
        filter_spec = split_dot(segment, forward_parts)
        return (grad_spec, conj_times(grad_spec, filter_spec, block_len), first_col)

    own_spec = split_dot(conv_input, head_parts)
    roll_table = jnp.concatenate([inverse[:, block_len:], inverse[:, :block_len]], axis=1)

    def add_block(state, grad_block, block_idx):
        mid_acc, lag_acc = state
        grad_spec, mid_piece, first_col = mid_term(grad_block, block_idx)
        lag_piece = spectral_dot(conj_times(own_spec, grad_spec, block_len), roll_table)
        previous = lax.dynamic_slice_in_dim(lag_acc, first_col, span_len, 1)
        lag_acc = lax.dynamic_update_slice_in_dim(lag_acc, previous + lag_piece, first_col, 1)
        return (mid_acc + mid_piece, lag_acc)

    init_state = (
        jnp.zeros((channels, span_len), jnp.float32),
        jnp.zeros((channels, shards * block_len + block_len), jnp.float32),
    )
    piece = lax.all_gather(conv_grad, "ctx", axis=1, tiled=True)
    blocks_in = piece.shape[1] // block_len
    stacked = jnp.moveaxis(piece.reshape(channels, blocks_in, block_len), 1, 0)
    indices = jnp.arange(blocks_in, dtype=jnp.int32)

    def step_one(carry, item):
        grad_block, block_idx = item
        result = lax.cond(
            block_idx >= own_index,
            lambda inner: add_block(inner, grad_block, block_idx),
            lambda inner: inner,
            carry,
        )
        return (result, None)

    result, unused = lax.scan(step_one, init_state, (stacked, indices))
    mid_acc, lag_acc = result
    lag_part = lag_acc[:, block_len:] * (1.0 / math.sqrt(shards * block_len))
    filter_grad = lax.psum_scatter(lag_part, "ctx", scatter_dimension=1, tiled=True)
    mid_table = inverse[:, 1 : block_len + 1][:, ::-1]
    mid_grad = (
        spectral_dot(mid_acc, mid_table) + skip_bias[:, None] * conv_grad.astype(jnp.float32)
    ).astype(jnp.bfloat16)
    taps = short_weight.shape[1]
    edge_rows = from_behind(mid_grad[:, : taps - 1], "ctx", -1)
    extended = jnp.concatenate([mid_grad, edge_rows], axis=1).astype(jnp.float32)
    input_grad = jnp.zeros((channels, block_len), jnp.float32)
    for tap_index in range(taps):
        input_grad = (
            input_grad
            + short_weight[:, tap_index : tap_index + 1]
            * extended[:, tap_index : tap_index + block_len]
        )
    return (input_grad.astype(jnp.bfloat16), filter_grad)


LANES = 128
SUBLANES = 8


def exchange_kernel(
    shards,
    input_ref,
    gate_ref,
    grad_ref,
    filter_ref,
    skip_ref,
    short_ref,
    input_grad_ref,
    filter_grad_ref,
    local,
    send_in,
    recv_in,
    rows,
    products,
    send_out,
    recv_out,
    load_sem,
    send_in_sem,
    recv_in_sem,
    send_out_sem,
    recv_out_sem,
):
    me = lax.axis_index("ctx")
    channels = local.shape[1]
    owned = channels // shards
    taps = short_ref.shape[0]
    scale = 1.0 / math.sqrt(shards * LANES)

    loads = [
        pltpu.make_async_copy(source, local.at[slot], load_sem.at[slot])
        for slot, source in enumerate((gate_ref, grad_ref, filter_ref, input_ref))
    ]
    for load in loads:
        load.start()
    barrier = pltpu.get_barrier_semaphore()
    for step in range(1, shards):
        pl.semaphore_signal(
            barrier,
            inc=1,
            device_id={"ctx": lax.rem(me + step, shards)},
            device_id_type=pl.DeviceIdType.MESH,
        )
    products[:, :, shards * SUBLANES :, :] = jnp.zeros(
        products.shape[:2] + (products.shape[2] - shards * SUBLANES, LANES), jnp.float32
    )
    for load in loads:
        load.wait()

    lane = lax.broadcasted_iota(jnp.int32, (LANES, LANES), 1)
    depth = lax.broadcasted_iota(jnp.int32, (LANES, LANES), 0)

    mirror = jnp.where(lane + depth == LANES - 1, 1.0, 0.0).astype(jnp.bfloat16)
    conv_grad = local[0].astype(jnp.float32) * local[1].astype(jnp.float32)
    filter_rows = jnp.dot(local[2], mirror, preferred_element_type=jnp.float32)
    input_rows = jnp.dot(local[3], mirror, preferred_element_type=jnp.float32)
    for peer in range(shards):
        own = slice(peer * owned, (peer + 1) * owned)
        tile = [conv_grad[own], filter_rows[own], input_rows[own]]
        tile.append(jnp.zeros((send_in.shape[1] - 3 * owned, LANES), jnp.float32))
        send_in[peer] = jnp.concatenate(tile, axis=0).astype(jnp.bfloat16)

    def sending(send, recv, send_sem, recv_sem, step):
        peer = lax.rem(me + step, shards)
        return pltpu.make_async_remote_copy(
            src_ref=send.at[peer],
            dst_ref=recv.at[me],
            send_sem=send_sem.at[step],
            recv_sem=recv_sem.at[step],
            device_id={"ctx": peer},
            device_id_type=pl.DeviceIdType.MESH,
        )

    def arriving(send, recv, send_sem, recv_sem, step):
        peer = lax.rem(me + shards - step, shards)
        return pltpu.make_async_remote_copy(
            src_ref=send.at[peer],
            dst_ref=recv.at[peer],
            send_sem=send_sem.at[step],
            recv_sem=recv_sem.at[step],
            device_id={"ctx": peer},
            device_id_type=pl.DeviceIdType.MESH,
        )

    first = (send_in, recv_in, send_in_sem, recv_in_sem)
    second = (send_out, recv_out, send_out_sem, recv_out_sem)

    pl.semaphore_wait(barrier, shards - 1)
    for step in range(1, shards):
        sending(*first, step).start()
    recv_in[me] = send_in[me]
    for step in range(1, shards):
        arriving(*first, step).wait_recv()
    rows[...] = recv_in[...].astype(jnp.float32)

    inside = lane <= depth
    edge = lax.broadcasted_iota(jnp.int32, (shards, LANES), 1)
    block = lax.broadcasted_iota(jnp.int32, (shards, LANES), 0)
    for slot in range(owned):
        weights = jnp.concatenate(
            [rows[:, owned + slot, :], rows[:, 2 * owned + slot, :]], axis=0
        ).astype(jnp.bfloat16)
        turned = []
        for part in range(shards):
            whole = jnp.broadcast_to(rows[part, slot : slot + 1, :], (LANES, LANES))
            turned.append(pltpu.roll(whole, 1, 1, stride=1, stride_axis=0))
        turned.append(jnp.zeros((LANES, LANES), jnp.float32))
        hankel = jnp.concatenate(
            [
                jnp.where(inside, turned[part], turned[part + 1]).astype(jnp.bfloat16)
                for part in range(shards)
            ],
            axis=1,
        )
        product = jnp.dot(weights, hankel, preferred_element_type=jnp.float32)
        for part in range(shards):
            piece = product[:, part * LANES : (part + 1) * LANES]
            at = slice(part * SUBLANES, (part + 1) * SUBLANES)
            products[slot, 0, at, :] = piece[:shards]
            products[slot, 1, at, :] = piece[shards:]

        def gathered(which):
            total = products[slot, which, pl.ds(0, shards, stride=SUBLANES), :]
            for part in range(1, shards):
                total = total + products[
                    slot, which, pl.ds(part * (SUBLANES + 1), shards, stride=SUBLANES), :
                ]
            return total

        channel = me * owned + slot
        mid = gathered(0) + skip_ref[channel] * rows[:, slot, :]
        mid = mid.astype(jnp.bfloat16).astype(jnp.float32)
        total = short_ref[0, channel] * mid
        for tap in range(1, taps):
            ahead = pltpu.roll(mid, LANES - tap, 1)
            carried = jnp.where(block < shards - 1, pltpu.roll(ahead, shards - 1, 0), 0.0)
            total = total + short_ref[tap, channel] * jnp.where(
                edge < LANES - tap, ahead, carried
            )
        send_out[:, slot, :] = total
        send_out[:, owned + slot, :] = gathered(1) * scale

    for step in range(1, shards):
        sending(*second, step).start()
    recv_out[me] = send_out[me]
    for step in range(1, shards):
        arriving(*second, step).wait_recv()
    for peer in range(0, shards, 2):
        at = slice(peer * owned, (peer + 2) * owned)
        input_grad_ref[at, :] = jnp.concatenate(
            [recv_out[peer, :owned], recv_out[peer + 1, :owned]], axis=0
        ).astype(jnp.bfloat16)
        filter_grad_ref[at, :] = jnp.concatenate(
            [recv_out[peer, owned:], recv_out[peer + 1, owned:]], axis=0
        )
    for step in range(1, shards):
        sending(*first, step).wait_send()
        sending(*second, step).wait_send()


def exchange_device(conv_input, gate_value, out_grad, long_filter, skip_bias, short_weight):
    channels, block_len = conv_input.shape
    shards = lax.axis_size("ctx")
    owned = channels // shards
    any_spec = pl.BlockSpec(memory_space=pl.ANY)
    smem_spec = pl.BlockSpec(memory_space=pltpu.SMEM)
    vmem_spec = pl.BlockSpec(memory_space=pltpu.VMEM)
    return pl.pallas_call(
        functools.partial(exchange_kernel, shards),
        out_shape=(
            jax.ShapeDtypeStruct((channels, block_len), jnp.bfloat16),
            jax.ShapeDtypeStruct((channels, block_len), jnp.float32),
        ),
        in_specs=[any_spec] * 4 + [smem_spec] * 2,
        out_specs=(vmem_spec, vmem_spec),
        scratch_shapes=[
            pltpu.VMEM((4, channels, LANES), jnp.bfloat16),
            pltpu.VMEM((shards, 16, LANES), jnp.bfloat16),
            pltpu.VMEM((shards, 16, LANES), jnp.bfloat16),
            pltpu.VMEM((shards, 16, LANES), jnp.float32),
            pltpu.VMEM((owned, 2, 2 * shards * SUBLANES, LANES), jnp.float32),
            pltpu.VMEM((shards, 2 * owned, LANES), jnp.float32),
            pltpu.VMEM((shards, 2 * owned, LANES), jnp.float32),
            pltpu.SemaphoreType.DMA((4,)),
            pltpu.SemaphoreType.DMA((shards,)),
            pltpu.SemaphoreType.DMA((shards,)),
            pltpu.SemaphoreType.DMA((shards,)),
            pltpu.SemaphoreType.DMA((shards,)),
        ],
        compiler_params=pltpu.CompilerParams(collective_id=0, has_side_effects=True),
    )(conv_input, gate_value, out_grad, long_filter, skip_bias, short_weight.T)


def per_device(*args):
    channels, block_len = args[0].shape
    shards = lax.axis_size("ctx")
    if block_len == LANES and shards == SUBLANES and channels == 4 * shards:
        return exchange_device(*args)
    return general_device(*args)


def solution(mesh):
    placed = (
        P("ch", "ctx"),
        P("ch", "ctx"),
        P("ch", "ctx"),
        P("ch", "ctx"),
        P("ch"),
        P("ch", None),
    )
    return jax.shard_map(
        per_device,
        mesh=mesh,
        in_specs=placed,
        out_specs=(P("ch", "ctx"), P("ch", "ctx")),
        check_vma=False,
    )
```

```python
import functools
import math

import jax
import jax.numpy as jnp
from jax import lax
from jax.experimental import pallas as pl
from jax.experimental.pallas import tpu as pltpu
from jax.sharding import PartitionSpec as P

LANES = 128
GROUP = 8


def gather_kernel(
    shards,
    input_ref,
    gate_ref,
    grad_ref,
    filter_ref,
    skip_ref,
    short_ref,
    input_grad_ref,
    filter_grad_ref,
    local,
    skip_row,
    short_rows,
    grads,
    pairs,
    sums,
    halo,
    shifted,
    load_sem,
    grad_send,
    grad_recv,
    pair_send,
    pair_recv,
):
    me = lax.axis_index("ctx")
    channels = local.shape[1]
    taps = short_rows.shape[0]
    last = shards - 1

    barrier = pltpu.get_barrier_semaphore()

    @pl.loop(me + 1, shards)
    def _(peer):
        pl.semaphore_signal(
            barrier, inc=1, device_id={"ctx": peer}, device_id_type=pl.DeviceIdType.MESH
        )

    loads = [
        pltpu.make_async_copy(source, target, load_sem.at[slot])
        for slot, (source, target) in enumerate(
            (
                (gate_ref, local.at[0]),
                (grad_ref, local.at[1]),
                (filter_ref, local.at[2]),
                (input_ref, local.at[3]),
                (skip_ref, skip_row),
                (short_ref, short_rows),
            )
        )
    ]
    for load in loads:
        load.start()
    grads[shards] = jnp.zeros((channels, LANES), jnp.bfloat16)
    sums[...] = jnp.zeros_like(sums)
    halo[...] = jnp.zeros_like(halo)
    shifted[...] = jnp.zeros_like(shifted)
    lane = lax.broadcasted_iota(jnp.int32, (LANES, LANES), 1)
    depth = lax.broadcasted_iota(jnp.int32, (LANES, LANES), 0)
    mirror = jnp.where(lane + depth == LANES - 1, 1.0, 0.0).astype(jnp.bfloat16)
    ahead = lane + depth >= LANES - 1

    def grad_copy(source, target):
        return pltpu.make_async_remote_copy(
            src_ref=grads.at[source],
            dst_ref=grads.at[source],
            send_sem=grad_send.at[target],
            recv_sem=grad_recv.at[source],
            device_id={"ctx": target},
            device_id_type=pl.DeviceIdType.MESH,
        )

    def pair_copy(source, target):
        return pltpu.make_async_remote_copy(
            src_ref=pairs.at[source],
            dst_ref=pairs.at[source],
            send_sem=pair_send.at[target],
            recv_sem=pair_recv.at[source],
            device_id={"ctx": target},
            device_id_type=pl.DeviceIdType.MESH,
        )

    loads[0].wait()
    loads[1].wait()
    grads[me] = (local[0].astype(jnp.float32) * local[1].astype(jnp.float32)).astype(jnp.bfloat16)

    @pl.when(me > 0)
    def _():
        pl.semaphore_wait(barrier, me)

    @pl.loop(0, me)
    def _(peer):
        grad_copy(me, peer).start()

    loads[2].wait()
    loads[3].wait()
    both = jnp.concatenate([local[2], local[3]], axis=0)
    pairs[me] = jnp.dot(both, mirror, preferred_element_type=jnp.float32).astype(jnp.bfloat16)

    @pl.loop(0, jnp.minimum(me, shards - me))
    def _(peer):
        pair_copy(me, peer).start()

    loads[4].wait()
    loads[5].wait()
    rows8 = lax.broadcasted_iota(jnp.int32, (2 * GROUP, LANES), 0) % GROUP
    lane_row = lax.broadcasted_iota(jnp.int32, (channels, LANES), 1)

    def step(lag, carry):
        now = me + lag
        after = now + 1

        @pl.when(after < shards)
        def _():
            grad_copy(after, after).wait_recv()

        @pl.when(jnp.logical_and(after < shards, after < shards - me))
        def _():
            pair_copy(me, after).start()

        @pl.when(lag != me)
        def _():
            pair_copy(lag, lag).wait_recv()

        grad_now = grads[now].astype(jnp.float32)
        grad_next = grads[after].astype(jnp.float32)
        pair = pairs[lag]
        plain = jnp.dot(pair[:channels], mirror, preferred_element_type=jnp.float32)
        halo[0] += plain * grad_next
        turn = plain
        for tap in range(1, taps - 1):
            turn = pltpu.roll(plain, tap, 1)
            halo[tap] += jnp.where(lane_row < tap, shifted[tap], turn) * grad_next
            shifted[tap] = turn
        pair = pair.astype(jnp.float32)
        for group in range(channels // GROUP):
            at = slice(group * GROUP, (group + 1) * GROUP)
            stack = jnp.concatenate([pair[:channels][at], pair[channels:][at]], axis=0)
            weights, hankel = [], []
            for item in range(GROUP):
                row = slice(group * GROUP + item, group * GROUP + item + 1)
                weights.append(jnp.where(rows8 == item, stack, 0.0).astype(jnp.bfloat16))
                mixed = jnp.where(
                    ahead,
                    jnp.broadcast_to(grad_now[row], (LANES, LANES)),
                    jnp.broadcast_to(grad_next[row], (LANES, LANES)),
                )
                hankel.append(
                    pltpu.roll(mixed, 1, 1, stride=1, stride_axis=0).astype(jnp.bfloat16)
                )
            sums[group] += jnp.dot(
                jnp.concatenate(weights, axis=1),
                jnp.concatenate(hankel, axis=0),
                preferred_element_type=jnp.float32,
            )
        return carry

    lax.fori_loop(0, shards - me, step, 0)

    wide = skip_row.shape[1]
    eye = lax.broadcasted_iota(jnp.int32, (channels, wide), 0) == lax.broadcasted_iota(
        jnp.int32, (channels, wide), 1
    )

    def column(row):
        return jnp.sum(jnp.where(eye, row, 0.0), axis=1, keepdims=True)

    skip = column(skip_row[...])
    own = grads[me].astype(jnp.float32)
    ahead_grad = grads[me + 1].astype(jnp.float32)

    def rounded(value):
        return value.astype(jnp.bfloat16).astype(jnp.float32)

    groups = channels // GROUP
    mid = rounded(
        jnp.concatenate([sums[group, :GROUP] for group in range(groups)], axis=0) + skip * own
    )
    scale = 1.0 / math.sqrt(shards * LANES)
    filter_grad_ref[...] = scale * jnp.concatenate(
        [sums[group, GROUP:] for group in range(groups)], axis=0
    )
    edge = [
        rounded(
            jnp.sum(halo[tap], axis=1, keepdims=True) + skip * ahead_grad[:, tap : tap + 1]
        )
        for tap in range(taps - 1)
    ]
    total = column(short_rows[0:1, :]) * mid
    for tap in range(1, taps):
        moved = pltpu.roll(mid, LANES - tap, 1)
        for reach in range(tap):
            moved = jnp.where(lane_row == LANES - tap + reach, edge[reach], moved)
        total = total + column(short_rows[tap : tap + 1, :]) * moved
    input_grad_ref[...] = total.astype(jnp.bfloat16)

    @pl.loop(0, me)
    def _(peer):
        grad_copy(me, peer).wait_send()

    @pl.loop(0, shards - me)
    def _(peer):
        @pl.when(peer != me)
        def _():
            pair_copy(me, peer).wait_send()


def per_device(conv_input, gate_value, out_grad, long_filter, skip_bias, short_weight):
    channels, block_len = conv_input.shape
    taps = short_weight.shape[1]
    shards = lax.axis_size("ctx")
    any_spec = pl.BlockSpec(memory_space=pl.ANY)
    vmem_spec = pl.BlockSpec(memory_space=pltpu.VMEM)
    return pl.pallas_call(
        functools.partial(gather_kernel, shards),
        out_shape=(
            jax.ShapeDtypeStruct((channels, block_len), jnp.bfloat16),
            jax.ShapeDtypeStruct((channels, block_len), jnp.float32),
        ),
        in_specs=[any_spec] * 6,
        out_specs=(vmem_spec, vmem_spec),
        scratch_shapes=[
            pltpu.VMEM((4, channels, LANES), jnp.bfloat16),
            pltpu.VMEM((1, channels), jnp.float32),
            pltpu.VMEM((taps, channels), jnp.float32),
            pltpu.VMEM((shards + 1, channels, LANES), jnp.bfloat16),
            pltpu.VMEM((shards, 2 * channels, LANES), jnp.bfloat16),
            pltpu.VMEM((channels // GROUP, 2 * GROUP, LANES), jnp.float32),
            pltpu.VMEM((taps - 1, channels, LANES), jnp.float32),
            pltpu.VMEM((taps - 1, channels, LANES), jnp.float32),
            pltpu.SemaphoreType.DMA((6,)),
            pltpu.SemaphoreType.DMA((shards,)),
            pltpu.SemaphoreType.DMA((shards,)),
            pltpu.SemaphoreType.DMA((shards,)),
            pltpu.SemaphoreType.DMA((shards,)),
        ],
        compiler_params=pltpu.CompilerParams(collective_id=0, has_side_effects=True),
    )(
        conv_input,
        gate_value,
        out_grad,
        long_filter,
        skip_bias.reshape(1, channels),
        short_weight.T,
    )


def solution(mesh):
    placed = (
        P("ch", "ctx"),
        P("ch", "ctx"),
        P("ch", "ctx"),
        P("ch", "ctx"),
        P("ch"),
        P("ch", None),
    )
    return jax.shard_map(
        per_device,
        mesh=mesh,
        in_specs=placed,
        out_specs=(P("ch", "ctx"), P("ch", "ctx")),
        check_vma=False,
    )
```

```python
import functools
import math

import jax
import jax.numpy as jnp
from jax import lax
from jax.experimental import pallas as pl
from jax.experimental.pallas import tpu as pltpu
from jax.sharding import PartitionSpec as P

LANES = 128
GROUP = 8
EARLY = 4


def gather_kernel(
    shards,
    input_ref,
    gate_ref,
    grad_ref,
    filter_ref,
    skip_ref,
    short_ref,
    input_grad_ref,
    filter_grad_ref,
    local,
    skip_row,
    short_rows,
    grads,
    pairs,
    sums,
    halo,
    shifted,
    load_sem,
    grad_send,
    grad_recv,
    pair_send,
    pair_recv,
    entered,
):
    me = lax.axis_index("ctx")
    channels = local.shape[1]
    taps = short_rows.shape[0]
    last = shards - 1

    loads = [
        pltpu.make_async_copy(source, target, load_sem.at[slot])
        for slot, (source, target) in enumerate(
            (
                (gate_ref, local.at[0]),
                (grad_ref, local.at[1]),
                (filter_ref, local.at[2]),
                (input_ref, local.at[3]),
                (skip_ref, skip_row),
                (short_ref, short_rows),
            )
        )
    ]
    for load in loads:
        load.start()
    barrier = pltpu.get_barrier_semaphore()

    @pl.loop(me + 1, shards)
    def _(peer):
        pl.semaphore_signal(
            barrier, inc=1, device_id={"ctx": peer}, device_id_type=pl.DeviceIdType.MESH
        )

    @pl.when(me > 0)
    def _():
        pl.semaphore_wait(barrier, me)

    @pl.loop(0, jnp.minimum(me, shards - me))
    def _(peer):
        pl.semaphore_signal(
            entered.at[me], inc=1, device_id={"ctx": peer}, device_id_type=pl.DeviceIdType.MESH
        )

    grads[shards] = jnp.zeros((channels, LANES), jnp.bfloat16)
    sums[...] = jnp.zeros_like(sums)
    halo[...] = jnp.zeros_like(halo)
    shifted[...] = jnp.zeros_like(shifted)
    lane = lax.broadcasted_iota(jnp.int32, (LANES, LANES), 1)
    depth = lax.broadcasted_iota(jnp.int32, (LANES, LANES), 0)
    mirror = jnp.where(lane + depth == LANES - 1, 1.0, 0.0).astype(jnp.bfloat16)
    ahead = lane + depth >= LANES - 1

    def grad_copy(source, target):
        return pltpu.make_async_remote_copy(
            src_ref=grads.at[source],
            dst_ref=grads.at[source],
            send_sem=grad_send.at[target],
            recv_sem=grad_recv.at[source],
            device_id={"ctx": target},
            device_id_type=pl.DeviceIdType.MESH,
        )

    def pair_copy(source, target):
        return pltpu.make_async_remote_copy(
            src_ref=pairs.at[source],
            dst_ref=pairs.at[source],
            send_sem=pair_send.at[target],
            recv_sem=pair_recv.at[source],
            device_id={"ctx": target},
            device_id_type=pl.DeviceIdType.MESH,
        )

    loads[0].wait()
    loads[1].wait()
    grads[me] = (local[0].astype(jnp.float32) * local[1].astype(jnp.float32)).astype(jnp.bfloat16)

    @pl.when(me > 0)
    def _():
        grad_copy(me, 0).start()

    loads[2].wait()
    loads[3].wait()
    both = jnp.concatenate([local[2], local[3]], axis=0)
    pairs[me] = jnp.dot(both, mirror, preferred_element_type=jnp.float32).astype(jnp.bfloat16)

    @pl.loop(0, jnp.minimum(me, shards - me))
    def _(peer):
        pair_copy(me, peer).start()

    @pl.loop(1, me)
    def _(peer):
        grad_copy(me, peer).start()

    def push_up(peer):
        @pl.when(peer < shards - me)
        def _():
            pl.semaphore_wait(entered.at[peer], 1)
            pair_copy(me, peer).start()

    @pl.loop(me + 1, me + 1 + EARLY)
    def _(peer):
        push_up(peer)

    loads[4].wait()
    loads[5].wait()
    rows8 = lax.broadcasted_iota(jnp.int32, (2 * GROUP, LANES), 0) % GROUP
    lane_row = lax.broadcasted_iota(jnp.int32, (channels, LANES), 1)

    def step(lag, carry):
        now = me + lag
        after = now + 1

        @pl.when(after < shards)
        def _():
            grad_copy(after, after).wait_recv()

        push_up(after + EARLY)

        @pl.when(lag != me)
        def _():
            pair_copy(lag, lag).wait_recv()

        grad_now = grads[now].astype(jnp.float32)
        grad_next = grads[after].astype(jnp.float32)
        pair = pairs[lag]
        plain = jnp.dot(pair[:channels], mirror, preferred_element_type=jnp.float32)
        halo[0] += plain * grad_next
        turn = plain
        for tap in range(1, taps - 1):
            turn = pltpu.roll(plain, tap, 1)
            halo[tap] += jnp.where(lane_row < tap, shifted[tap], turn) * grad_next
            shifted[tap] = turn
        pair = pair.astype(jnp.float32)
        for group in range(channels // GROUP):
            at = slice(group * GROUP, (group + 1) * GROUP)
            stack = jnp.concatenate([pair[:channels][at], pair[channels:][at]], axis=0)
            weights, hankel = [], []
            for item in range(GROUP):
                row = slice(group * GROUP + item, group * GROUP + item + 1)
                weights.append(jnp.where(rows8 == item, stack, 0.0).astype(jnp.bfloat16))
                mixed = jnp.where(
                    ahead,
                    jnp.broadcast_to(grad_now[row], (LANES, LANES)),
                    jnp.broadcast_to(grad_next[row], (LANES, LANES)),
                )
                hankel.append(
                    pltpu.roll(mixed, 1, 1, stride=1, stride_axis=0).astype(jnp.bfloat16)
                )
            sums[group] += jnp.dot(
                jnp.concatenate(weights, axis=1),
                jnp.concatenate(hankel, axis=0),
                preferred_element_type=jnp.float32,
            )
        return carry

    lax.fori_loop(0, shards - me, step, 0)

    wide = skip_row.shape[1]
    eye = lax.broadcasted_iota(jnp.int32, (channels, wide), 0) == lax.broadcasted_iota(
        jnp.int32, (channels, wide), 1
    )

    def column(row):
        return jnp.sum(jnp.where(eye, row, 0.0), axis=1, keepdims=True)

    skip = column(skip_row[...])
    own = grads[me].astype(jnp.float32)
    ahead_grad = grads[me + 1].astype(jnp.float32)

    def rounded(value):
        return value.astype(jnp.bfloat16).astype(jnp.float32)

    groups = channels // GROUP
    mid = rounded(
        jnp.concatenate([sums[group, :GROUP] for group in range(groups)], axis=0) + skip * own
    )
    scale = 1.0 / math.sqrt(shards * LANES)
    filter_grad_ref[...] = scale * jnp.concatenate(
        [sums[group, GROUP:] for group in range(groups)], axis=0
    )
    edge = [
        rounded(
            jnp.sum(halo[tap], axis=1, keepdims=True) + skip * ahead_grad[:, tap : tap + 1]
        )
        for tap in range(taps - 1)
    ]
    total = column(short_rows[0:1, :]) * mid
    for tap in range(1, taps):
        moved = pltpu.roll(mid, LANES - tap, 1)
        for reach in range(tap):
            moved = jnp.where(lane_row == LANES - tap + reach, edge[reach], moved)
        total = total + column(short_rows[tap : tap + 1, :]) * moved
    input_grad_ref[...] = total.astype(jnp.bfloat16)

    @pl.loop(0, me)
    def _(peer):
        grad_copy(me, peer).wait_send()

    @pl.loop(0, shards - me)
    def _(peer):
        @pl.when(peer != me)
        def _():
            pair_copy(me, peer).wait_send()


def per_device(conv_input, gate_value, out_grad, long_filter, skip_bias, short_weight):
    channels, block_len = conv_input.shape
    taps = short_weight.shape[1]
    shards = lax.axis_size("ctx")
    any_spec = pl.BlockSpec(memory_space=pl.ANY)
    vmem_spec = pl.BlockSpec(memory_space=pltpu.VMEM)
    return pl.pallas_call(
        functools.partial(gather_kernel, shards),
        out_shape=(
            pltpu.VMEM((channels, block_len), jnp.bfloat16),
            pltpu.VMEM((channels, block_len), jnp.float32),
        ),
        in_specs=[any_spec] * 6,
        out_specs=(vmem_spec, vmem_spec),
        scratch_shapes=[
            pltpu.VMEM((4, channels, LANES), jnp.bfloat16),
            pltpu.VMEM((1, channels), jnp.float32),
            pltpu.VMEM((taps, channels), jnp.float32),
            pltpu.VMEM((shards + 1, channels, LANES), jnp.bfloat16),
            pltpu.VMEM((shards, 2 * channels, LANES), jnp.bfloat16),
            pltpu.VMEM((channels // GROUP, 2 * GROUP, LANES), jnp.float32),
            pltpu.VMEM((taps - 1, channels, LANES), jnp.float32),
            pltpu.VMEM((taps - 1, channels, LANES), jnp.float32),
            pltpu.SemaphoreType.DMA((6,)),
            pltpu.SemaphoreType.DMA((shards,)),
            pltpu.SemaphoreType.DMA((shards,)),
            pltpu.SemaphoreType.DMA((shards,)),
            pltpu.SemaphoreType.DMA((shards,)),
            pltpu.SemaphoreType.REGULAR((shards,)),
        ],
        compiler_params=pltpu.CompilerParams(
            collective_id=0,
            has_side_effects=True,
        ),
    )(
        conv_input,
        gate_value,
        out_grad,
        long_filter,
        skip_bias.reshape(1, channels),
        short_weight.T,
    )


def solution(mesh):
    placed = (
        P("ch", "ctx"),
        P("ch", "ctx"),
        P("ch", "ctx"),
        P("ch", "ctx"),
        P("ch"),
        P("ch", None),
    )
    return jax.shard_map(
        per_device,
        mesh=mesh,
        in_specs=placed,
        out_specs=(P("ch", "ctx"), P("ch", "ctx")),
        check_vma=False,
    )
```

```python
import functools
import math

import jax
import jax.numpy as jnp
from jax import lax
from jax.experimental import pallas as pl
from jax.experimental.pallas import tpu as pltpu
from jax.sharding import PartitionSpec as P

LANES = 128
GROUP = 8
EARLY = 4


def gather_kernel(
    shards,
    input_ref,
    gate_ref,
    grad_ref,
    filter_ref,
    skip_ref,
    short_ref,
    input_grad_ref,
    filter_grad_ref,
    local,
    skip_row,
    short_rows,
    grads,
    pairs,
    sums,
    halo,
    shifted,
    load_sem,
    grad_send,
    grad_recv,
    pair_send,
    pair_recv,
    entered,
):
    me = lax.axis_index("ctx")
    channels = local.shape[1]
    taps = short_rows.shape[0]
    last = shards - 1

    loads = [
        pltpu.make_async_copy(source, target, load_sem.at[slot])
        for slot, (source, target) in enumerate(
            (
                (gate_ref, local.at[0]),
                (grad_ref, local.at[1]),
                (filter_ref, local.at[2]),
                (input_ref, local.at[3]),
                (skip_ref, skip_row),
                (short_ref, short_rows),
            )
        )
    ]
    for load in loads:
        load.start()
    barrier = pltpu.get_barrier_semaphore()

    @pl.loop(me + 1, shards)
    def _(peer):
        pl.semaphore_signal(
            barrier, inc=1, device_id={"ctx": peer}, device_id_type=pl.DeviceIdType.MESH
        )

    @pl.when(me > 0)
    def _():
        pl.semaphore_wait(barrier, me)

    @pl.loop(0, jnp.minimum(me, shards - me))
    def _(peer):
        pl.semaphore_signal(
            entered.at[me], inc=1, device_id={"ctx": peer}, device_id_type=pl.DeviceIdType.MESH
        )

    grads[shards] = jnp.zeros((channels, LANES), jnp.bfloat16)
    sums[...] = jnp.zeros_like(sums)
    halo[...] = jnp.zeros_like(halo)
    shifted[...] = jnp.zeros_like(shifted)
    lane = lax.broadcasted_iota(jnp.int32, (LANES, LANES), 1)
    depth = lax.broadcasted_iota(jnp.int32, (LANES, LANES), 0)
    mirror = jnp.where(lane + depth == LANES - 1, 1.0, 0.0).astype(jnp.bfloat16)
    ahead = lane + depth >= LANES - 1

    def grad_copy(source, target):
        return pltpu.make_async_remote_copy(
            src_ref=grads.at[source],
            dst_ref=grads.at[source],
            send_sem=grad_send.at[target],
            recv_sem=grad_recv.at[source],
            device_id={"ctx": target},
            device_id_type=pl.DeviceIdType.MESH,
        )

    def pair_copy(source, target):
        return pltpu.make_async_remote_copy(
            src_ref=pairs.at[source],
            dst_ref=pairs.at[source],
            send_sem=pair_send.at[target],
            recv_sem=pair_recv.at[source],
            device_id={"ctx": target},
            device_id_type=pl.DeviceIdType.MESH,
        )

    loads[0].wait()
    loads[1].wait()
    grads[me] = (local[0].astype(jnp.float32) * local[1].astype(jnp.float32)).astype(jnp.bfloat16)

    @pl.when(me > 0)
    def _():
        grad_copy(me, 0).start()

    loads[2].wait()
    loads[3].wait()
    both = jnp.concatenate([local[2], local[3]], axis=0)
    pairs[me] = jnp.dot(both, mirror, preferred_element_type=jnp.float32).astype(jnp.bfloat16)

    @pl.loop(0, jnp.minimum(me, shards - me))
    def _(peer):
        pair_copy(me, peer).start()

    @pl.loop(1, me)
    def _(peer):
        grad_copy(me, peer).start()

    def push_up(peer):
        @pl.when(peer < shards - me)
        def _():
            pl.semaphore_wait(entered.at[peer], 1)
            pair_copy(me, peer).start()

    @pl.loop(me + 1, me + 1 + EARLY)
    def _(peer):
        push_up(peer)

    loads[4].wait()
    loads[5].wait()
    rows8 = lax.broadcasted_iota(jnp.int32, (2 * GROUP, LANES), 0) % GROUP
    lane_row = lax.broadcasted_iota(jnp.int32, (channels, LANES), 1)

    def step(lag, carry):
        now = me + lag
        after = now + 1

        @pl.when(after < shards)
        def _():
            grad_copy(after, after).wait_recv()

        push_up(after + EARLY)

        @pl.when(lag != me)
        def _():
            pair_copy(lag, lag).wait_recv()

        grad_now = grads[now].astype(jnp.float32)
        grad_next = grads[after].astype(jnp.float32)
        pair = pairs[lag]
        plain = jnp.dot(pair[:channels], mirror, preferred_element_type=jnp.float32)
        halo[0] += plain * grad_next
        turn = plain
        for tap in range(1, taps - 1):
            turn = pltpu.roll(plain, tap, 1)
            halo[tap] += jnp.where(lane_row < tap, shifted[tap], turn) * grad_next
            shifted[tap] = turn
        pair = pair.astype(jnp.float32)
        for group in range(channels // GROUP):
            at = slice(group * GROUP, (group + 1) * GROUP)
            stack = jnp.concatenate([pair[:channels][at], pair[channels:][at]], axis=0)
            weights, hankel = [], []
            for item in range(GROUP):
                row = slice(group * GROUP + item, group * GROUP + item + 1)
                weights.append(jnp.where(rows8 == item, stack, 0.0).astype(jnp.bfloat16))
                mixed = jnp.where(
                    ahead,
                    jnp.broadcast_to(grad_now[row], (LANES, LANES)),
                    jnp.broadcast_to(grad_next[row], (LANES, LANES)),
                )
                hankel.append(
                    pltpu.roll(mixed, 1, 1, stride=1, stride_axis=0).astype(jnp.bfloat16)
                )
            sums[group] += jnp.dot(
                jnp.concatenate(weights, axis=1),
                jnp.concatenate(hankel, axis=0),
                preferred_element_type=jnp.float32,
            )
        return carry

    lax.fori_loop(0, shards - me, step, 0)

    wide = skip_row.shape[1]
    eye = lax.broadcasted_iota(jnp.int32, (channels, wide), 0) == lax.broadcasted_iota(
        jnp.int32, (channels, wide), 1
    )

    def column(row):
        return jnp.sum(jnp.where(eye, row, 0.0), axis=1, keepdims=True)

    skip = column(skip_row[...])
    own = grads[me].astype(jnp.float32)
    ahead_grad = grads[me + 1].astype(jnp.float32)

    def rounded(value):
        return value.astype(jnp.bfloat16).astype(jnp.float32)

    groups = channels // GROUP
    mid = rounded(
        jnp.concatenate([sums[group, :GROUP] for group in range(groups)], axis=0) + skip * own
    )
    scale = 1.0 / math.sqrt(shards * LANES)
    filter_grad_ref[...] = scale * jnp.concatenate(
        [sums[group, GROUP:] for group in range(groups)], axis=0
    )
    edge = [
        rounded(
            jnp.sum(halo[tap], axis=1, keepdims=True) + skip * ahead_grad[:, tap : tap + 1]
        )
        for tap in range(taps - 1)
    ]
    total = column(short_rows[0:1, :]) * mid
    for tap in range(1, taps):
        moved = pltpu.roll(mid, LANES - tap, 1)
        for reach in range(tap):
            moved = jnp.where(lane_row == LANES - tap + reach, edge[reach], moved)
        total = total + column(short_rows[tap : tap + 1, :]) * moved
    input_grad_ref[...] = total.astype(jnp.bfloat16)

    @pl.loop(0, me)
    def _(peer):
        grad_copy(me, peer).wait_send()

    @pl.loop(0, shards - me)
    def _(peer):
        @pl.when(peer != me)
        def _():
            pair_copy(me, peer).wait_send()


def place_kernel(small_ref, wide_ref, small_out, wide_out, sem):
    copies = [
        pltpu.make_async_copy(source, target, sem.at[slot])
        for slot, (source, target) in enumerate(((wide_ref, wide_out), (small_ref, small_out)))
    ]
    for copy in copies:
        copy.start()
    for copy in copies:
        copy.wait()


def placed_copy(small, wide):
    any_spec = pl.BlockSpec(memory_space=pl.ANY)
    vmem_spec = pl.BlockSpec(memory_space=pltpu.VMEM)
    return pl.pallas_call(
        place_kernel,
        out_shape=(
            jax.ShapeDtypeStruct(small.shape, small.dtype),
            jax.ShapeDtypeStruct(wide.shape, wide.dtype),
        ),
        in_specs=[vmem_spec] * 2,
        out_specs=(any_spec, any_spec),
        scratch_shapes=[pltpu.SemaphoreType.DMA((2,))],
    )(*(pltpu.with_memory_space_constraint(value, pltpu.VMEM) for value in (small, wide)))


def per_device(conv_input, gate_value, out_grad, long_filter, skip_bias, short_weight):
    channels, block_len = conv_input.shape
    taps = short_weight.shape[1]
    shards = lax.axis_size("ctx")
    any_spec = pl.BlockSpec(memory_space=pl.ANY)
    vmem_spec = pl.BlockSpec(memory_space=pltpu.VMEM)
    results = pl.pallas_call(
        functools.partial(gather_kernel, shards),
        out_shape=(
            pltpu.VMEM((channels, block_len), jnp.bfloat16),
            pltpu.VMEM((channels, block_len), jnp.float32),
        ),
        in_specs=[any_spec] * 6,
        out_specs=(vmem_spec, vmem_spec),
        scratch_shapes=[
            pltpu.VMEM((4, channels, LANES), jnp.bfloat16),
            pltpu.VMEM((1, channels), jnp.float32),
            pltpu.VMEM((taps, channels), jnp.float32),
            pltpu.VMEM((shards + 1, channels, LANES), jnp.bfloat16),
            pltpu.VMEM((shards, 2 * channels, LANES), jnp.bfloat16),
            pltpu.VMEM((channels // GROUP, 2 * GROUP, LANES), jnp.float32),
            pltpu.VMEM((taps - 1, channels, LANES), jnp.float32),
            pltpu.VMEM((taps - 1, channels, LANES), jnp.float32),
            pltpu.SemaphoreType.DMA((6,)),
            pltpu.SemaphoreType.DMA((shards,)),
            pltpu.SemaphoreType.DMA((shards,)),
            pltpu.SemaphoreType.DMA((shards,)),
            pltpu.SemaphoreType.DMA((shards,)),
            pltpu.SemaphoreType.REGULAR((shards,)),
        ],
        compiler_params=pltpu.CompilerParams(
            collective_id=0,
            has_side_effects=True,
        ),
    )(
        conv_input,
        gate_value,
        out_grad,
        long_filter,
        skip_bias.reshape(1, channels),
        short_weight.T,
    )
    return placed_copy(*results)


def solution(mesh):
    placed = (
        P("ch", "ctx"),
        P("ch", "ctx"),
        P("ch", "ctx"),
        P("ch", "ctx"),
        P("ch"),
        P("ch", None),
    )
    return jax.shard_map(
        per_device,
        mesh=mesh,
        in_specs=placed,
        out_specs=(P("ch", "ctx"), P("ch", "ctx")),
        check_vma=False,
    )
```

```python
import functools
import math

import jax
import jax.numpy as jnp
from jax import lax
from jax.experimental import pallas as pl
from jax.experimental.pallas import tpu as pltpu
from jax.sharding import PartitionSpec as P

LANES = 128
GROUP = 8
EARLY = 4


def gather_kernel(
    shards,
    input_ref,
    gate_ref,
    grad_ref,
    filter_ref,
    skip_ref,
    short_ref,
    input_grad_ref,
    filter_grad_ref,
    local,
    skip_row,
    short_rows,
    grads,
    pairs,
    sums,
    halo,
    shifted,
    load_sem,
    grad_send,
    grad_recv,
    pair_send,
    pair_recv,
    entered,
):
    me = lax.axis_index("ctx")
    channels = local.shape[1]
    taps = short_rows.shape[0]
    last = shards - 1

    loads = [
        pltpu.make_async_copy(source, target, load_sem.at[slot])
        for slot, (source, target) in enumerate(
            (
                (gate_ref, local.at[0]),
                (grad_ref, local.at[1]),
                (filter_ref, local.at[2]),
                (input_ref, local.at[3]),
                (skip_ref, skip_row),
                (short_ref, short_rows),
            )
        )
    ]
    for load in loads:
        load.start()
    barrier = pltpu.get_barrier_semaphore()

    @pl.loop(me + 1, shards)
    def _(peer):
        pl.semaphore_signal(
            barrier, inc=1, device_id={"ctx": peer}, device_id_type=pl.DeviceIdType.MESH
        )

    @pl.when(me > 0)
    def _():
        pl.semaphore_wait(barrier, me)

    @pl.loop(0, jnp.minimum(me, shards - me))
    def _(peer):
        pl.semaphore_signal(
            entered.at[me], inc=1, device_id={"ctx": peer}, device_id_type=pl.DeviceIdType.MESH
        )

    grads[shards] = jnp.zeros((channels, LANES), jnp.bfloat16)
    sums[...] = jnp.zeros_like(sums)
    halo[...] = jnp.zeros_like(halo)
    shifted[...] = jnp.zeros_like(shifted)
    lane = lax.broadcasted_iota(jnp.int32, (LANES, LANES), 1)
    depth = lax.broadcasted_iota(jnp.int32, (LANES, LANES), 0)
    mirror = jnp.where(lane + depth == LANES - 1, 1.0, 0.0).astype(jnp.bfloat16)
    own_part = lane <= depth

    def grad_copy(source, target):
        return pltpu.make_async_remote_copy(
            src_ref=grads.at[source],
            dst_ref=grads.at[source],
            send_sem=grad_send.at[target],
            recv_sem=grad_recv.at[source],
            device_id={"ctx": target},
            device_id_type=pl.DeviceIdType.MESH,
        )

    def pair_copy(source, target):
        return pltpu.make_async_remote_copy(
            src_ref=pairs.at[source],
            dst_ref=pairs.at[source],
            send_sem=pair_send.at[target],
            recv_sem=pair_recv.at[source],
            device_id={"ctx": target},
            device_id_type=pl.DeviceIdType.MESH,
        )

    loads[0].wait()
    loads[1].wait()
    grads[me] = (local[0].astype(jnp.float32) * local[1].astype(jnp.float32)).astype(jnp.bfloat16)

    @pl.when(me > 0)
    def _():
        grad_copy(me, 0).start()

    loads[2].wait()
    loads[3].wait()
    both = jnp.concatenate([local[2], local[3]], axis=0)
    pairs[me] = jnp.dot(both, mirror, preferred_element_type=jnp.float32).astype(jnp.bfloat16)

    @pl.loop(0, jnp.minimum(me, shards - me))
    def _(peer):
        pair_copy(me, peer).start()

    @pl.loop(1, me)
    def _(peer):
        grad_copy(me, peer).start()

    def push_up(peer):
        @pl.when(peer < shards - me)
        def _():
            pl.semaphore_wait(entered.at[peer], 1)
            pair_copy(me, peer).start()

    @pl.loop(me + 1, me + 1 + EARLY)
    def _(peer):
        push_up(peer)

    loads[4].wait()
    loads[5].wait()
    rows8 = lax.broadcasted_iota(jnp.int32, (2 * GROUP, LANES), 0) % GROUP
    lane_row = lax.broadcasted_iota(jnp.int32, (channels, LANES), 1)

    wide = skip_row.shape[1]
    eye = lax.broadcasted_iota(jnp.int32, (channels, wide), 0) == lax.broadcasted_iota(
        jnp.int32, (channels, wide), 1
    )

    def column(row):
        return jnp.sum(jnp.where(eye, row, 0.0), axis=1, keepdims=True)

    skip = column(skip_row[...])
    short = [column(short_rows[tap : tap + 1, :]) for tap in range(taps)]

    def step(lag, carry):
        now = me + lag

        @pl.when(lag > 0)
        def _():
            grad_copy(now, now).wait_recv()
            push_up(now + EARLY)

        @pl.when(lag != me)
        def _():
            pair_copy(lag, lag).wait_recv()

        grad_now = grads[now].astype(jnp.float32)
        pair = pairs[lag].astype(jnp.float32)
        before = pairs[jnp.maximum(lag - 1, 0)].astype(jnp.float32)
        before = jnp.where(lag > 0, before, 0.0)
        plain = jnp.dot(
            before[:channels].astype(jnp.bfloat16), mirror, preferred_element_type=jnp.float32
        )
        halo[0] += plain * grad_now
        for tap in range(1, taps - 1):
            turn = pltpu.roll(plain, tap, 1)
            halo[tap] += jnp.where(lane_row < tap, shifted[tap], turn) * grad_now
            shifted[tap] = turn
        for group in range(channels // GROUP):
            at = slice(group * GROUP, (group + 1) * GROUP)
            stacks = [
                jnp.concatenate([source[:channels][at], source[channels:][at]], axis=0)
                for source in (pair, before)
            ]
            weights, hankel = [], []
            for item in range(GROUP):
                row = slice(group * GROUP + item, group * GROUP + item + 1)
                turned = pltpu.roll(
                    jnp.broadcast_to(grad_now[row], (LANES, LANES)), 1, 1, stride=1, stride_axis=0
                )
                for stack, kept in zip(stacks, (own_part, ~own_part)):
                    weights.append(jnp.where(rows8 == item, stack, 0.0).astype(jnp.bfloat16))
                    hankel.append(jnp.where(kept, turned, 0.0).astype(jnp.bfloat16))
            sums[group] += jnp.dot(
                jnp.concatenate(weights, axis=1),
                jnp.concatenate(hankel, axis=0),
                preferred_element_type=jnp.float32,
            )
        return carry

    lax.fori_loop(0, shards - me, step, 0)

    own = grads[me].astype(jnp.float32)
    ahead_grad = grads[me + 1].astype(jnp.float32)

    def rounded(value):
        return value.astype(jnp.bfloat16).astype(jnp.float32)

    groups = channels // GROUP
    mid = rounded(
        jnp.concatenate([sums[group, :GROUP] for group in range(groups)], axis=0) + skip * own
    )
    scale = 1.0 / math.sqrt(shards * LANES)
    filter_grad_ref[...] = scale * jnp.concatenate(
        [sums[group, GROUP:] for group in range(groups)], axis=0
    )
    edge = [
        rounded(
            jnp.sum(halo[tap], axis=1, keepdims=True) + skip * ahead_grad[:, tap : tap + 1]
        )
        for tap in range(taps - 1)
    ]
    total = short[0] * mid
    for tap in range(1, taps):
        moved = pltpu.roll(mid, LANES - tap, 1)
        for reach in range(tap):
            moved = jnp.where(lane_row == LANES - tap + reach, edge[reach], moved)
        total = total + short[tap] * moved
    input_grad_ref[...] = total.astype(jnp.bfloat16)

    @pl.loop(0, me)
    def _(peer):
        grad_copy(me, peer).wait_send()

    @pl.loop(0, shards - me)
    def _(peer):
        @pl.when(peer != me)
        def _():
            pair_copy(me, peer).wait_send()


def place_kernel(small_ref, wide_ref, small_out, wide_out, sem):
    copies = [
        pltpu.make_async_copy(source, target, sem.at[slot])
        for slot, (source, target) in enumerate(((wide_ref, wide_out), (small_ref, small_out)))
    ]
    for copy in copies:
        copy.start()
    for copy in copies:
        copy.wait()


def placed_copy(small, wide):
    any_spec = pl.BlockSpec(memory_space=pl.ANY)
    vmem_spec = pl.BlockSpec(memory_space=pltpu.VMEM)
    return pl.pallas_call(
        place_kernel,
        out_shape=(
            jax.ShapeDtypeStruct(small.shape, small.dtype),
            jax.ShapeDtypeStruct(wide.shape, wide.dtype),
        ),
        in_specs=[vmem_spec] * 2,
        out_specs=(any_spec, any_spec),
        scratch_shapes=[pltpu.SemaphoreType.DMA((2,))],
    )(*(pltpu.with_memory_space_constraint(value, pltpu.VMEM) for value in (small, wide)))


def per_device(conv_input, gate_value, out_grad, long_filter, skip_bias, short_weight):
    channels, block_len = conv_input.shape
    taps = short_weight.shape[1]
    shards = lax.axis_size("ctx")
    any_spec = pl.BlockSpec(memory_space=pl.ANY)
    vmem_spec = pl.BlockSpec(memory_space=pltpu.VMEM)
    results = pl.pallas_call(
        functools.partial(gather_kernel, shards),
        out_shape=(
            pltpu.VMEM((channels, block_len), jnp.bfloat16),
            pltpu.VMEM((channels, block_len), jnp.float32),
        ),
        in_specs=[any_spec] * 6,
        out_specs=(vmem_spec, vmem_spec),
        scratch_shapes=[
            pltpu.VMEM((4, channels, LANES), jnp.bfloat16),
            pltpu.VMEM((1, channels), jnp.float32),
            pltpu.VMEM((taps, channels), jnp.float32),
            pltpu.VMEM((shards + 1, channels, LANES), jnp.bfloat16),
            pltpu.VMEM((shards, 2 * channels, LANES), jnp.bfloat16),
            pltpu.VMEM((channels // GROUP, 2 * GROUP, LANES), jnp.float32),
            pltpu.VMEM((taps - 1, channels, LANES), jnp.float32),
            pltpu.VMEM((taps - 1, channels, LANES), jnp.float32),
            pltpu.SemaphoreType.DMA((6,)),
            pltpu.SemaphoreType.DMA((shards,)),
            pltpu.SemaphoreType.DMA((shards,)),
            pltpu.SemaphoreType.DMA((shards,)),
            pltpu.SemaphoreType.DMA((shards,)),
            pltpu.SemaphoreType.REGULAR((shards,)),
        ],
        compiler_params=pltpu.CompilerParams(
            collective_id=0,
            has_side_effects=True,
        ),
    )(
        conv_input,
        gate_value,
        out_grad,
        long_filter,
        skip_bias.reshape(1, channels),
        short_weight.T,
    )
    return placed_copy(*results)


def solution(mesh):
    placed = (
        P("ch", "ctx"),
        P("ch", "ctx"),
        P("ch", "ctx"),
        P("ch", "ctx"),
        P("ch"),
        P("ch", None),
    )
    return jax.shard_map(
        per_device,
        mesh=mesh,
        in_specs=placed,
        out_specs=(P("ch", "ctx"), P("ch", "ctx")),
        check_vma=False,
    )
```
